512 devices in a mesh: dp: 64 (over x, z), expert: 8 (over y, core).
Axes of the slice: x: 4, y: 4, z: 16, core: 2. Of those that a mesh axis runs over, the one named last changes fastest.
Arguments:
- tokens: bfloat16 [8192, 2048], P('dp'), may hold values from -6 to 6
- routes: int32 [8192, 8], P('dp'), may hold values from 0 to 63, all different within a row; in each aligned block of 128 rows (0 to 127, 128 to 255, ...) at most 16 rows name the same one
- kept_mask: int32 [8192, 8], P('dp'), may hold values from 0 to 1, as said below
- gate_probs: float32 [8192, 8], P('dp'), may hold values from 0.05 to 0.5
- output_grad: bfloat16 [8192, 2048], P('dp'), may hold values from -96 to 96
- w_gate: bfloat16 [64, 2048, 1024], P('dp', None, 'expert'), may hold values from -0.125 to 0.125
- w_up: bfloat16 [64, 2048, 1024], P('dp', None, 'expert'), may hold values from -0.125 to 0.125
- w_down: bfloat16 [64, 1024, 2048], P('dp', 'expert'), may hold values from -0.1875 to 0.1875
Outputs:
- output: bfloat16 [8192, 2048], P('dp', 'expert')
- input_grad: bfloat16 [8192, 2048], P('dp', 'expert')
- grad_gate: bfloat16 [64, 2048, 1024], P('dp', None, 'expert')
- grad_up: bfloat16 [64, 2048, 1024], P('dp', None, 'expert')
- grad_down: bfloat16 [64, 1024, 2048], P('dp', 'expert')
The draws below stay inside these ranges and needn't reach their ends.
Inputs may be any that keep to these rules, and one draw needn't show every extreme that they name: `routes`: each row names 8 different experts, and the 128 rows of each index of dp name every expert exactly 16 times. `kept_mask`: the share of kept entries varies along the tokens.
All inputs are finite; a program needn't handle non-finite values.
Results may differ from the reference program's by a relative error of at most 0.0064.
Values may be sent and summed in bfloat16 or wider, within the bound.
A program may use at most 64 MiB of HBM per device.

```python
import math
import jax
import jax.numpy as jnp
import numpy as np
from jax import lax

D = 2048
HIDDEN_SIZE = 1024
TOPK = 8
TOK = 128
EXPERTS = 64
TOKENS = 8192
CAP = 16
SLOTS = 1024
N_DP = 64


def draw_kept_mask(key, part):
    row_ids = jnp.arange(TOKENS, dtype=jnp.int32)[:, None]
    level = 300 + 650 * row_ids // TOKENS
    ticket = jax.random.randint(key, (TOKENS, TOPK), 0, 1000, dtype=jnp.int32)
    return (ticket < level).astype(jnp.int32)


def steps_of(stream_key, shape, pieces, smallest, top_value):
    loudness, own = 1.0, jax.random.fold_in(stream_key, 6)
    for axis_at, shards_of in pieces:
        heights = jnp.exp(jax.random.uniform(jax.random.fold_in(own, axis_at), (shards_of,), jnp.float32, smallest / len(pieces), top_value / len(pieces)))
        loudness = loudness * jnp.repeat(heights, shape[axis_at] // shards_of).reshape([-1 if axis == axis_at else 1 for axis in range(len(shape))])
    return loudness


def assign_block(key, own, number, rows, number_of, top, most, slope):
    sequence = jax.random.permutation(key, number_of)
    heavy_load, ordinary = load_shares(number_of, rows * top, most, slope, True), load_shares(number_of, rows * top, most, slope, False)
    places = jnp.arange(number_of)

    def named(tallies, rotation):
        used = int((tallies > 0).sum())
        fixed = max(1, used // 4)
        shifted = fixed + (places - fixed + rotation * (used - fixed)) % max(1, number_of - fixed)
        return jnp.zeros((number_of,), jnp.int32).at[sequence[jnp.where(places < fixed, places, shifted)]].set(jnp.asarray(tallies, jnp.int32))

    tallies = jnp.where(number % 4 == 0, named(heavy_load, number // 4), named(ordinary, number - number // 4 - 1))
    mixed = jax.random.permutation(jax.random.fold_in(own, 3), number_of)
    donor, taker = mixed[0:number_of // 2 * 2:2], mixed[1:number_of // 2 * 2:2]
    slack = jnp.minimum(tallies[donor] - 1, most - tallies[taker]) // 2
    slack = jnp.where((donor == sequence[0]) | (taker == sequence[0]) | (tallies[taker] == 0), 0, jnp.maximum(slack, 0))
    shifted = jax.random.randint(jax.random.fold_in(own, 4), (number_of // 2,), 0, 1 << 20) % (slack + 1)
    tallies = tallies.at[donor].add(-shifted).at[taker].add(shifted)
    items = jnp.searchsorted(jnp.cumsum(tallies), jnp.arange(rows * top), side="right").astype(jnp.int32)
    table = items.reshape(top, rows).T
    table = table[jax.random.permutation(jax.random.fold_in(own, 1), rows)]
    rotation = jax.random.randint(jax.random.fold_in(own, 2), (rows, 1), 0, top)
    return jnp.take_along_axis(table, (jnp.arange(top)[None, :] + rotation) % top, axis=1)


def load_shares(count, total, most, slope, full):
    loads = [(1 << 20) // math.isqrt(rank ** slope) + 1 for rank in range(1, count + 1)]
    largest = most if full else min(most, max(-(-total // count), total * loads[0] // sum(loads)))
    least = 1 if total - largest >= count - 1 else 0
    given, spare = [largest] + [least] * (count - 1), total - largest - least * (count - 1)
    while spare > 0:
        candidates = [i for i in range(1, count) if given[i] < largest] or [i for i in range(1, count) if given[i] < most]
        whole, budget = sum([loads[i] for i in candidates]), spare
        for i in candidates:
            more = min(most - given[i], max(1, budget * loads[i] // whole), spare)
            given[i] = given[i] + more
            spare = spare - more
    return np.array(given)


def scatter_about(rng, shape, spread, bound, pieces=(), kind=jnp.bfloat16):
    factor_of = steps_of(rng, shape, pieces, -0.22, 0.18) if pieces else 1.0
    result = jax.random.normal(rng, shape, jnp.float32) * spread * factor_of
    return jnp.minimum(jnp.maximum(result, -bound), bound).astype(kind)


def setup_inputs(seed: int = 0) -> dict:
    seeds = jax.random.split(jax.random.key(seed), 9)
    tokens = scatter_about(seeds[0], (TOKENS, D), 1.0, 6.0, ((0, 64),))
    routes_keys = jax.random.split(jax.random.fold_in(seeds[1], 1), TOKENS // TOK)
    routes_turns = jax.random.permutation(jax.random.fold_in(seeds[1], 3), TOKENS // TOK)
    routes = jax.vmap(lambda own, number: assign_block(jax.random.fold_in(seeds[1], 2), own, number, TOK, EXPERTS, TOPK, CAP, 0))(routes_keys, routes_turns).reshape((TOKENS, TOPK))
    kept_mask = draw_kept_mask(jax.random.fold_in(seeds[8], 71), 0)
    gate_probs = jnp.clip(0.05 + 0.45 * jax.random.uniform(seeds[3], (TOKENS, TOPK), jnp.float32) ** steps_of(seeds[3], (TOKENS, TOPK), ((0, 64),), -0.2, 0.2), 0.05, 0.5)
    output_grad = scatter_about(seeds[4], (TOKENS, D), 16.0, 96.0, ((0, 64),))
    w_gate = scatter_about(seeds[5], (EXPERTS, D, HIDDEN_SIZE), D ** -0.5, 0.125, ((0, 64), (2, 8)))
    w_up = scatter_about(seeds[6], (EXPERTS, D, HIDDEN_SIZE), D ** -0.5, 0.125, ((0, 64), (2, 8)))
    w_down = scatter_about(seeds[7], (EXPERTS, HIDDEN_SIZE, D), HIDDEN_SIZE ** -0.5, 0.1875, ((0, 64), (1, 8)))
    return {"tokens": tokens, "routes": routes, "kept_mask": kept_mask, "gate_probs": gate_probs, "output_grad": output_grad, "w_gate": w_gate, "w_up": w_up, "w_down": w_down}


def silu_parts(gate_val):
    sigmoid_val = jax.nn.sigmoid(gate_val)
    return gate_val * sigmoid_val, sigmoid_val * (1.0 + gate_val * (1.0 - sigmoid_val))


def reference(tokens, routes, kept_mask, gate_probs, output_grad, w_gate, w_up, w_down):
    pair_count = TOKENS * TOPK
    flat_routes = routes.reshape(N_DP, TOK * TOPK)
    onehot = (flat_routes[:, :, None] == jnp.arange(EXPERTS, dtype=jnp.int32)[None, None, :]).astype(jnp.int32)
    before = jnp.cumsum(onehot, axis=1) - onehot
    slot_index = jnp.sum(before * onehot, axis=2)
    shard_base = (jnp.arange(N_DP, dtype=jnp.int32) * CAP)[:, None]
    dest_index = (flat_routes * SLOTS + shard_base + slot_index).reshape(pair_count).astype(jnp.int32)
    source = jnp.zeros((pair_count,), jnp.int32).at[dest_index].set(jnp.arange(pair_count, dtype=jnp.int32))
    keep_float = kept_mask.reshape(pair_count).astype(jnp.float32)
    weight_flat = keep_float * gate_probs.reshape(pair_count)
    kept_count = jnp.sum(onehot.astype(jnp.float32) * keep_float.reshape(N_DP, TOK * TOPK, 1), axis=(0, 1))
    src_token = (source // TOPK).reshape(EXPERTS, SLOTS)
    src_keep = keep_float[source].reshape(EXPERTS, SLOTS)
    src_weight = weight_flat[source].reshape(EXPERTS, SLOTS)

    def one_expert(bundle):
        gate_w, up_w, down_w, token_ids, keep_rows, weight_rows, expert_count = bundle
        expert_in = (tokens[token_ids].astype(jnp.float32) * keep_rows[:, None]).astype(jnp.bfloat16)
        cot_rows = (output_grad[token_ids].astype(jnp.float32) * weight_rows[:, None]).astype(jnp.bfloat16)
        gate_val = jnp.dot(expert_in, gate_w, preferred_element_type=jnp.float32)
        up_val = jnp.dot(expert_in, up_w, preferred_element_type=jnp.float32)
        act_val, act_slope = silu_parts(gate_val)
        hidden = (act_val * up_val).astype(jnp.bfloat16)
        expert_out = jnp.dot(hidden, down_w, preferred_element_type=jnp.float32).astype(jnp.bfloat16)
        d_hidden = jnp.dot(cot_rows, down_w.T, preferred_element_type=jnp.float32)
        d_gate = (d_hidden * up_val * act_slope).astype(jnp.bfloat16)
        d_up = (d_hidden * act_val).astype(jnp.bfloat16)
        inv_count = 1.0 / jnp.maximum(expert_count, 1.0)
        grad_down = (jnp.dot(hidden.T, cot_rows, preferred_element_type=jnp.float32) * inv_count).astype(jnp.bfloat16)
        grad_gate = (jnp.dot(expert_in.T, d_gate, preferred_element_type=jnp.float32) * inv_count).astype(jnp.bfloat16)
        grad_up = (jnp.dot(expert_in.T, d_up, preferred_element_type=jnp.float32) * inv_count).astype(jnp.bfloat16)
        d_rows = (jnp.dot(d_gate, gate_w.T, preferred_element_type=jnp.float32)
                  + jnp.dot(d_up, up_w.T, preferred_element_type=jnp.float32)).astype(jnp.bfloat16)
        return expert_out, d_rows, grad_gate, grad_up, grad_down

    expert_out, d_rows, grad_gate, grad_up, grad_down = lax.map(
        one_expert, (w_gate, w_up, w_down, src_token, src_keep, src_weight, kept_count))
    out_rows = expert_out.reshape(pair_count, D)[dest_index].astype(jnp.float32) * weight_flat[:, None]
    output = jnp.sum(out_rows.reshape(TOKENS, TOPK, D), axis=1).astype(jnp.bfloat16)
    grad_rows = d_rows.reshape(pair_count, D)[dest_index].astype(jnp.float32) * keep_float[:, None]
    input_grad = jnp.sum(grad_rows.reshape(TOKENS, TOPK, D), axis=1).astype(jnp.bfloat16)
    return output, input_grad, grad_gate, grad_up, grad_down
```

```python
import functools

import jax
import jax.numpy as jnp
from jax import lax
from jax.experimental import pallas as pl
from jax.experimental.pallas import tpu as pltpu
from jax.sharding import Mesh
from jax.sharding import PartitionSpec as P

MESH = pl.DeviceIdType.MESH
F32 = jnp.float32
BF16 = jnp.bfloat16

NX, NZ, NY, NC = 4, 16, 4, 2
NF = NY * NC
CH = 64
LAG = 4
NT = (((1,), (1,)), ((), ()))
TN = (((0,), (0,)), ((), ()))


def rdma(src, dst, send_sem, recv_sem, **where):
    return pltpu.make_async_remote_copy(
        src_ref=src,
        dst_ref=dst,
        send_sem=send_sem,
        recv_sem=recv_sem,
        device_id=where,
        device_id_type=MESH,
    )


def rows_of(s, off=0, size=CH):
    return pl.ds(pl.multiple_of(s * CH + off, 16), size)


def mod(v, n):
    return lax.rem(v + 2 * n, n)


def kernel(
    tok,
    grd,
    routes,
    kept,
    probs,
    wg,
    wu,
    wd,
    out,
    ing,
    ggate,
    gup,
    gdown,
    tbuf,
    rbuf,
    stg,
    xc,
    hdu,
    wgu,
    gu,
    dn,
    eo,
    ret,
    psend,
    precv,
    cst,
    crecv,
    local_sem,
    wgt_send,
    wgt_recv,
    z_send,
    z_recv,
    x_send,
    x_recv,
    c_send,
    c_recv,
    ag1_send,
    ag1_y,
    ag1_h,
    ag1_c,
    ag2_send,
    ag2_y,
    ag2_h,
    ag2_c,
    e_send,
    e_recv,
    p_send,
    p_recv,
):
    x = lax.axis_index("x")
    z = lax.axis_index("z")
    y = lax.axis_index("y")
    c = lax.axis_index("c")
    f = y * NC + c
    zp, zm = mod(z + 1, NZ), mod(z - 1, NZ)
    yp, ym, y2 = mod(y + 1, NY), mod(y - 1, NY), mod(y + 2, NY)
    oc = 1 - c
    width = out.shape[1]

    cols = pl.ds(pl.multiple_of(f * width, width), width)
    own_t = pltpu.make_async_copy(tok.at[:, cols], tbuf.at[z, :, pl.ds(0, width)], local_sem.at[0])
    own_g = pltpu.make_async_copy(grd.at[:, cols], tbuf.at[z, :, pl.ds(width, width)], local_sem.at[1])
    own_t.start()
    own_g.start()
    hid = wg.shape[1]
    side_g = pltpu.make_async_copy(wg, wgu.at[:, pl.ds(0, hid)], local_sem.at[2])
    side_u = pltpu.make_async_copy(wu, wgu.at[:, pl.ds(hid, hid)], local_sem.at[3])
    side_g.start()
    side_u.start()

    barrier = pltpu.get_barrier_semaphore()
    for where in [{"z": zp}, {"z": zm}] + [{"x": mod(x + d, NX)} for d in range(1, NX)]:
        pl.semaphore_signal(barrier, inc=1, device_id=where, device_id_type=MESH)
    for d in range(1, NF):
        to = mod(f + d, NF)
        pl.semaphore_signal(
            barrier, inc=1, device_id={"y": to // NC, "c": lax.rem(to, NC)}, device_id_type=MESH
        )

    nexp = NX * NZ
    tok_rows = routes.shape[1]
    rt = routes[...]
    e_iota = lax.broadcasted_iota(jnp.int32, (nexp, tok_rows), 0)
    named = jnp.zeros((nexp, tok_rows), F32)
    for k in range(8):
        named = named + jnp.where(rt[k : k + 1, :] == e_iota, 1.0, 0.0)
    before = lax.broadcasted_iota(jnp.int32, (tok_rows, tok_rows), 0) < lax.broadcasted_iota(
        jnp.int32, (tok_rows, tok_rows), 1
    )
    rank = jnp.dot(
        named.astype(BF16), jnp.where(before, 1.0, 0.0).astype(BF16), preferred_element_type=F32
    )
    kf = kept[...].astype(F32)
    weight = kf * probs[...]
    for k in range(8):
        slot = jnp.sum(jnp.where(rt[k : k + 1, :] == e_iota, rank, 0.0), axis=0, keepdims=True)
        dest = rt[k : k + 1, :].astype(F32) * 16.0 + slot
        rbuf[z, k : k + 1, :] = jnp.where(kf[k : k + 1, :] > 0.0, dest, -1.0)
        rbuf[z, 8 + k : 9 + k, :] = weight[k : k + 1, :]
    cst[...] = jnp.zeros_like(cst)

    pl.semaphore_wait(barrier, 2 + (NX - 1) + (NF - 1))
    own_t.wait()
    own_g.wait()

    def z_copies(direction, s, hop):
        to = zp if direction == 0 else zm
        return [
            rdma(buf.at[s], buf.at[s], z_send.at[direction, i], z_recv.at[direction, i, hop], z=to)
            for i, buf in enumerate((tbuf, rbuf))
        ]

    def z_start(direction, s, hop):
        for copy in z_copies(direction, s, hop):
            copy.start()

    def z_wait(direction, s, hop):
        for copy in z_copies(direction, s, hop):
            copy.wait_recv()

    z_start(0, z, 0)
    z_start(1, z, 0)

    def wblock(ref, b):
        at = pl.ds(pl.multiple_of(b * width, width), width)
        return ref.at[at, :] if ref is not wd else ref.at[:, at]

    def wplace(i, b):
        return (
            gu.at[b, :, pl.ds(0, hid)] if i == 0 else gu.at[b, :, pl.ds(hid, hid)] if i == 1 else dn.at[b]
        )

    for d in range(1, NF):
        to = mod(f + d, NF)
        for i, ref in enumerate((wg, wu, wd)):
            rdma(
                wblock(ref, to),
                wplace(i, f),
                wgt_send.at[i],
                wgt_recv.at[i, f],
                y=to // NC,
                c=lax.rem(to, NC),
            ).start()
    own_w = [
        pltpu.make_async_copy(wblock(ref, f), wplace(i, f), wgt_recv.at[i, f])
        for i, ref in enumerate((wg, wu, wd))
    ]
    for copy in own_w:
        copy.start()

    def selection(s):
        info = rbuf[s]
        r = lax.broadcasted_iota(jnp.int32, (CH, tok_rows), 0)
        name = ((r >> 4) * (NZ * 16) + (r & 15) + z * 16).astype(F32)
        hit = jnp.zeros((CH, tok_rows), F32)
        wgt = jnp.zeros((CH, tok_rows), F32)
        for k in range(8):
            same = info[k : k + 1, :] == name
            hit = hit + jnp.where(same, 1.0, 0.0)
            wgt = wgt + jnp.where(same, info[8 + k : 9 + k, :], 0.0)
        return hit, wgt

    def select_rows(s):
        hit, wgt = selection(s)
        picked = jnp.dot(hit.astype(BF16), tbuf[s], preferred_element_type=F32)
        scale = jnp.sum(wgt, axis=1, keepdims=True)
        stg[s, :, 0:width] = picked[:, :width].astype(BF16)
        stg[s, :, width:] = (picked[:, width:] * scale).astype(BF16)
        cst[...] += hit

    def x_copies(src, dst, send, recv, s):
        def part(v):
            return pl.ds(pl.multiple_of(v * 16, 16), 16)

        mine = pltpu.make_async_copy(src(s, x), dst(s, x), recv.at[s, x])
        others = []
        for d in range(1, NX):
            to = mod(x + d, NX)
            others.append(rdma(src(s, to), dst(s, x), send, recv.at[s, x], x=to))
        return mine, others

    def x_waits(src, dst, send, recv, s):
        pltpu.make_async_copy(src(s, x), dst(s, x), recv.at[s, x]).wait()
        for d in range(1, NX):
            frm = mod(x + d, NX)
            rdma(src(s, frm), dst(s, frm), send, recv.at[s, frm], x=frm).wait_recv()

    def stg_src(s, v):
        return stg.at[s, pl.ds(pl.multiple_of(v * 16, 16), 16), :]

    def xc_dst(s, v):
        return xc.at[f, pl.ds(pl.multiple_of(s * CH + v * 16, 16), 16), :]

    def x_send_rows(s):
        mine, others = x_copies(stg_src, xc_dst, x_send, x_recv, s)
        mine.start()
        for copy in others:
            copy.start()

    def x_wait_rows(s):
        x_waits(stg_src, xc_dst, x_send, x_recv, s)

    def gatherer(buf, send, ysem, hsem, csem):
        def own(s):
            here = buf.at[f, rows_of(s)]
            rdma(here, here, send.at[0], ysem.at[0, s], y=yp).start()
            rdma(here, here, send.at[1], ysem.at[1, s], y=ym).start()
            rdma(here, here, send.at[2], csem.at[0, s], c=oc).start()

        def forward(s):
            for i, (frm, to, off) in enumerate(((ym, yp, 0), (yp, ym, CH // 2))):
                b = frm * NC + c
                whole = buf.at[b, rows_of(s)]
                half = buf.at[b, rows_of(s, off, CH // 2)]
                rdma(whole, whole, send.at[i], ysem.at[i, s], y=frm).wait_recv()
                rdma(half, half, send.at[3 + i], hsem.at[i, s], y=to).start()
                rdma(whole, whole, send.at[5 + i], csem.at[1 + i, s], c=oc).start()

        def halves(s):
            b = y2 * NC + c
            whole = buf.at[b, rows_of(s)]
            for i, frm in enumerate((ym, yp)):
                half = buf.at[b, rows_of(s, i * (CH // 2), CH // 2)]
                rdma(half, half, send.at[3 + i], hsem.at[i, s], y=frm).wait_recv()
            rdma(whole, whole, send.at[7], csem.at[3, s], c=oc).start()

        def other_core(s):
            for i, yy in enumerate((y, ym, yp, y2)):
                whole = buf.at[yy * NC + oc, rows_of(s)]
                rdma(whole, whole, send.at[2], csem.at[i, s], c=oc).wait_recv()

        def drain():
            full = buf.at[f]
            half = buf.at[f, pl.ds(0, NZ * CH // 2)]
            for i in range(8):
                part = half if i in (3, 4) else full
                rdma(part, part, send.at[i], ysem.at[0, 0], c=oc).wait_send()

        return own, forward, halves, other_core, drain

    own1, forward1, halves1, other1, drain1 = gatherer(xc, ag1_send, ag1_y, ag1_h, ag1_c)
    own2, forward2, halves2, other2, drain2 = gatherer(hdu, ag2_send, ag2_y, ag2_h, ag2_c)

    side_g.wait()
    side_u.wait()

    def up_chunks(sa, sb):
        gate_up = jnp.zeros((2 * CH, 2 * hid), F32)
        d_hid = jnp.zeros((2 * CH, hid), F32)
        for b in range(NF):
            xs = jnp.concatenate([xc[b, rows_of(s), 0:width] for s in (sa, sb)], axis=0)
            cs = jnp.concatenate([xc[b, rows_of(s), width : 2 * width] for s in (sa, sb)], axis=0)
            gate_up += jnp.dot(xs, wgu[b * width : (b + 1) * width, :], preferred_element_type=F32)
            d_hid += lax.dot_general(
                cs, wd[:, b * width : (b + 1) * width], NT, preferred_element_type=F32
            )
        gate, up = gate_up[:, :hid], gate_up[:, hid:]
        sig = jax.nn.sigmoid(gate)
        act = gate * sig
        slope = sig * (1.0 + gate * (1.0 - sig))
        hidden = (act * up).astype(BF16)
        d_gate = (d_hid * up * slope).astype(BF16)
        d_up = (d_hid * act).astype(BF16)
        for i, s in enumerate((sa, sb)):
            part = slice(i * CH, (i + 1) * CH)
            hdu[f, rows_of(s), 0:hid] = hidden[part]
            hdu[f, rows_of(s), hid : 2 * hid] = d_gate[part]
            hdu[f, rows_of(s), 2 * hid : 3 * hid] = d_up[part]

    def pair(k):
        return mod(z - k, NZ), mod(z + 1 + k, NZ)

    half_ring = NZ // 2

    def step1(i, carry):
        sa, sb = pair(i)

        @pl.when(i < half_ring)
        def _():
            @pl.when(i >= 1)
            def _():
                z_wait(0, sa, i - 1)

                @pl.when(i <= half_ring - 2)
                def _():
                    z_start(0, sa, i)

            z_wait(1, sb, i)

            @pl.when(i <= half_ring - 2)
            def _():
                z_start(1, sb, i + 1)

            select_rows(sa)
            select_rows(sb)

        @pl.when((i >= 1) & (i < half_ring + 1))
        def _():
            for s in pair(i - 1):
                x_wait_rows(s)
                own1(s)

        @pl.when((i >= 2) & (i < half_ring + 2))
        def _():
            for s in pair(i - 2):
                forward1(s)

        @pl.when((i >= 3) & (i < half_ring + 3))
        def _():
            for s in pair(i - 3):
                halves1(s)

        @pl.when(i < half_ring)
        def _():
            x_send_rows(sa)
            x_send_rows(sb)

        @pl.when(i >= 4)
        def _():
            pa, pb = pair(i - 4)
            other1(pa)
            other1(pb)
            up_chunks(pa, pb)

        return carry

    lax.fori_loop(0, half_ring + LAG, step1, 0)

    def cst_src(s, v):
        return cst.at[pl.ds(pl.multiple_of(v * 16, 16), 16), :]

    def cst_dst(s, v):
        return crecv.at[v]

    c_mine, c_others = x_copies(cst_src, cst_dst, c_send, c_recv, 0)
    c_mine.start()
    for copy in c_others:
        copy.start()
    x_waits(cst_src, cst_dst, c_send, c_recv, 0)
    total = jnp.sum(jnp.sum(crecv[...], axis=0), axis=0, keepdims=True)
    count = jnp.sum(total, axis=1, keepdims=True)
    inv = 1.0 / jnp.maximum(count, 1.0)

    for copy in own_w:
        copy.wait()
    for d in range(1, NF):
        frm = mod(f + d, NF)
        for i, ref in enumerate((wg, wu, wd)):
            rdma(
                wblock(ref, frm),
                wplace(i, frm),
                wgt_send.at[i],
                wgt_recv.at[i, frm],
                y=frm // NC,
                c=lax.rem(frm, NC),
            ).wait_recv()

    def back_pair(m):
        return mod(z + half_ring - m, NZ), mod(z - (half_ring - 1) + m, NZ)

    def down_chunks(sa, sb):
        e_out = jnp.zeros((2 * CH, width), F32)
        d_row = jnp.zeros((2 * CH, width), F32)
        for b in range(NF):
            hs = jnp.concatenate([hdu[b, rows_of(s), 0:hid] for s in (sa, sb)], axis=0)
            ds = jnp.concatenate([hdu[b, rows_of(s), hid : 3 * hid] for s in (sa, sb)], axis=0)
            e_out += jnp.dot(hs, dn[b], preferred_element_type=F32)
            d_row += lax.dot_general(ds, gu[b], NT, preferred_element_type=F32)
        for i, s in enumerate((sa, sb)):
            part = slice(i * CH, (i + 1) * CH)
            eo[s, :, 0:width] = e_out[part].astype(BF16)
            eo[s, :, width:] = d_row[part].astype(BF16)

    def eo_src(s, v):
        return eo.at[s, pl.ds(pl.multiple_of(v * 16, 16), 16), :]

    def ret_dst(s, v):
        return ret.at[s, pl.ds(pl.multiple_of(v * 16, 16), 16), :]

    def contribution(s):
        hit, wgt = selection(s)
        high = wgt.astype(BF16)
        low = (wgt - high.astype(F32)).astype(BF16)
        back_o = ret[s, :, 0:width]
        back_d = ret[s, :, width:]
        part_o = lax.dot_general(
            jnp.concatenate([high, low], axis=0),
            jnp.concatenate([back_o, back_o], axis=0),
            TN,
            preferred_element_type=F32,
        )
        part_d = lax.dot_general(hit.astype(BF16), back_d, TN, preferred_element_type=F32)
        return part_o, part_d

    def p_copy(direction, m):
        to = zp if direction == 0 else zm
        return rdma(
            psend.at[direction, m],
            precv.at[direction, m],
            p_send.at[direction],
            p_recv.at[direction, m],
            z=to,
        )

    def add_and_store(direction, s, m, carried):
        part_o, part_d = contribution(s)
        if carried:
            part_o += precv[direction, m - 1, :, 0:width].astype(F32)
            part_d += precv[direction, m - 1, :, width:].astype(F32)
        psend[direction, m, :, 0:width] = part_o.astype(BF16)
        psend[direction, m, :, width:] = part_d.astype(BF16)

    def grads(b):
        at = pl.ds(pl.multiple_of(b * width, width), width)
        d_gu = lax.dot_general(
            xc[b, :, 0:width], hdu[f, :, hid : 3 * hid], TN, preferred_element_type=F32
        )
        ggate[at, :] = (d_gu[:, :hid] * inv).astype(BF16)
        gup[at, :] = (d_gu[:, hid:] * inv).astype(BF16)
        d_dn = lax.dot_general(
            hdu[f, :, 0:hid], xc[b, :, width : 2 * width], TN, preferred_element_type=F32
        )
        gdown[:, at] = (d_dn * inv).astype(BF16)

    def step2(i, carry):
        @pl.when(i < half_ring)
        def _():
            for s in back_pair(i):
                own2(s)

        @pl.when((i >= 1) & (i < half_ring + 1))
        def _():
            for s in back_pair(i - 1):
                forward2(s)

        @pl.when((i >= 2) & (i < half_ring + 2))
        def _():
            for s in back_pair(i - 2):
                halves2(s)

        @pl.when((i >= 3) & (i < half_ring + 3))
        def _():
            sa, sb = back_pair(i - 3)
            other2(sa)
            other2(sb)
            down_chunks(sa, sb)

        @pl.when((i >= 4) & (i < half_ring + 3))
        def _():
            m = i - 4
            sa, sb = back_pair(m)
            for s in (sa, sb):
                x_waits(eo_src, ret_dst, e_send, e_recv, s)

            @pl.when(m == 0)
            def _():
                add_and_store(0, sa, m, False)
                add_and_store(1, sb, m, False)

            @pl.when(m >= 1)
            def _():
                p_copy(0, m - 1).wait_recv()
                p_copy(1, m - 1).wait_recv()
                add_and_store(0, sa, m, True)
                add_and_store(1, sb, m, True)

            p_copy(0, m).start()
            p_copy(1, m).start()

        @pl.when((i >= 3) & (i < half_ring + 3))
        def _():
            for s in back_pair(i - 3):
                mine, others = x_copies(eo_src, ret_dst, e_send, e_recv, s)
                mine.start()
                for copy in others:
                    copy.start()

        @pl.when(i < half_ring)
        def _():
            grads(i)

        return carry

    lax.fori_loop(0, half_ring + 3, step2, 0)

    last = half_ring - 1
    sa, sb = back_pair(last)
    x_waits(eo_src, ret_dst, e_send, e_recv, sa)
    p_copy(0, last - 1).wait_recv()
    add_and_store(0, sa, last, True)
    p_copy(0, last).start()
    x_waits(eo_src, ret_dst, e_send, e_recv, sb)
    part_o, part_d = contribution(sb)
    p_copy(1, last - 1).wait_recv()
    part_o += precv[1, last - 1, :, 0:width].astype(F32)
    part_d += precv[1, last - 1, :, width:].astype(F32)
    p_copy(0, last).wait_recv()
    out[...] = (part_o + precv[0, last, :, 0:width].astype(F32)).astype(BF16)
    ing[...] = (part_d + precv[0, last, :, width:].astype(F32)).astype(BF16)

    drain1()
    drain2()
    for direction, hops in ((0, half_ring - 1), (1, half_ring)):
        to = zp if direction == 0 else zm
        for i, buf in enumerate((tbuf, rbuf)):
            part = buf.at[pl.ds(0, hops)]
            rdma(part, part, z_send.at[direction, i], z_recv.at[direction, i, 0], z=to).wait_send()
    x_part = NZ * (NX - 1) // NX
    for ref, sem in ((stg, x_send), (eo, e_send)):
        part = ref.at[pl.ds(0, x_part)]
        rdma(part, part, sem, x_recv.at[0, 0], x=mod(x + 1, NX)).wait_send()
    part = crecv.at[pl.ds(0, NX - 1)]
    rdma(part, part, c_send, c_recv.at[0, 0], x=mod(x + 1, NX)).wait_send()
    for direction, hops in ((0, half_ring), (1, half_ring - 1)):
        part = psend.at[direction, pl.ds(0, hops)]
        to = zp if direction == 0 else zm
        rdma(part, part, p_send.at[direction], p_recv.at[direction, 0], z=to).wait_send()
    for i, ref in enumerate((wg, wu, wd)):
        at = pl.ds(0, (NF - 1) * width)
        part = ref.at[at, :] if i < 2 else ref.at[:, at]
        rdma(part, part, wgt_send.at[i], wgt_recv.at[i, 0], c=oc).wait_send()


def per_device(tokens, routes, kept_mask, gate_probs, output_grad, w_gate, w_up, w_down):
    tok_rows, model = tokens.shape
    width = model // NF
    hid = w_gate.shape[2]
    wg, wu, wd = w_gate[0], w_up[0], w_down[0]
    vmem = pl.BlockSpec(memory_space=pltpu.VMEM)
    hbm = pl.BlockSpec(memory_space=pl.ANY)
    dma = pltpu.SemaphoreType.DMA
    gather_sems = [dma((8,)), dma((2, NZ)), dma((2, NZ)), dma((4, NZ))]
    outs = pl.pallas_call(
        kernel,
        out_shape=(
            jax.ShapeDtypeStruct((tok_rows, width), BF16),
            jax.ShapeDtypeStruct((tok_rows, width), BF16),
            jax.ShapeDtypeStruct(wg.shape, BF16),
            jax.ShapeDtypeStruct(wu.shape, BF16),
            jax.ShapeDtypeStruct(wd.shape, BF16),
        ),
        in_specs=[hbm, hbm] + [vmem] * 6,
        out_specs=[vmem] * 5,
        scratch_shapes=[
            pltpu.VMEM((NZ, tok_rows, 2 * width), BF16),
            pltpu.VMEM((NZ, 16, tok_rows), F32),
            pltpu.VMEM((NZ, CH, 2 * width), BF16),
            pltpu.VMEM((NF, NZ * CH, 2 * width), BF16),
            pltpu.VMEM((NF, NZ * CH, 3 * hid), BF16),
            pltpu.VMEM((model, 2 * hid), BF16),
            pltpu.VMEM((NF, width, 2 * hid), BF16),
            pltpu.VMEM((NF, hid, width), BF16),
            pltpu.VMEM((NZ, CH, 2 * width), BF16),
            pltpu.VMEM((NZ, CH, 2 * width), BF16),
            pltpu.VMEM((2, NZ // 2, tok_rows, 2 * width), BF16),
            pltpu.VMEM((2, NZ // 2, tok_rows, 2 * width), BF16),
            pltpu.VMEM((CH, tok_rows), F32),
            pltpu.VMEM((NX, 16, tok_rows), F32),
            dma((4,)),
            dma((3,)),
            dma((3, NF)),
            dma((2, 2)),
            dma((2, 2, NZ // 2)),
            dma(()),
            dma((NZ, NX)),
            dma(()),
            dma((1, NX)),
            *gather_sems,
            *gather_sems,
            dma(()),
            dma((NZ, NX)),
            dma((2,)),
            dma((2, NZ // 2)),
        ],
        compiler_params=pltpu.CompilerParams(
            collective_id=0, has_side_effects=True, vmem_limit_bytes=56 * 1024 * 1024
        ),
    )(tokens, output_grad, routes.T, kept_mask.T, gate_probs.T, wg, wu, wd)
    output, input_grad, g_gate, g_up, g_down = outs
    return output, input_grad, g_gate[None], g_up[None], g_down[None]


def solution(mesh):
    torus = Mesh(mesh.devices.reshape(NX, NZ, NY, NC), ("x", "z", "y", "c"))
    dp, expert = ("x", "z"), ("y", "c")
    return jax.shard_map(
        per_device,
        mesh=torus,
        in_specs=(
            P(dp, None),
            P(dp, None),
            P(dp, None),
            P(dp, None),
            P(dp, None),
            P(dp, None, expert),
            P(dp, None, expert),
            P(dp, expert, None),
        ),
        out_specs=(
            P(dp, expert),
            P(dp, expert),
            P(dp, None, expert),
            P(dp, None, expert),
            P(dp, expert, None),
        ),
        check_vma=False,
    )
```

```python
import functools

import jax
import jax.numpy as jnp
from jax import lax
from jax.experimental import pallas as pl
from jax.experimental.pallas import tpu as pltpu
from jax.sharding import Mesh
from jax.sharding import PartitionSpec as P

MESH = pl.DeviceIdType.MESH
F32 = jnp.float32
BF16 = jnp.bfloat16

NX, NZ, NY, NC = 4, 16, 4, 2
NF = NY * NC
CH = 64
LAG = 4
EARLY = 1
TN = (((0,), (0,)), ((), ()))


def rdma(src, dst, send_sem, recv_sem, **where):
    return pltpu.make_async_remote_copy(
        src_ref=src,
        dst_ref=dst,
        send_sem=send_sem,
        recv_sem=recv_sem,
        device_id=where,
        device_id_type=MESH,
    )


def rows_of(s, off=0, size=CH):
    return pl.ds(pl.multiple_of(s * CH + off, 16), size)


def mod(v, n):
    return lax.rem(v + 2 * n, n)


def kernel(
    tok,
    grd,
    routes_h,
    kept_h,
    probs_h,
    wg,
    wu,
    wd,
    out,
    ing,
    ggate,
    gup,
    gdown,
    tbuf,
    rbuf,
    stg,
    xc,
    hdu,
    wgu,
    gu,
    dn,
    eo,
    ret,
    psend,
    precv,
    cst,
    crecv,
    wdv,
    gg,
    gdn,
    inv_ref,
    pick_o,
    pick_d,
    wdt,
    gut,
    routes,
    kept,
    probs,
    local_sem,
    grad_sem,
    wgt_send,
    wgt_recv,
    z_send,
    z_recv,
    x_send,
    x_recv,
    c_send,
    c_recv,
    ag1_send,
    ag1_y,
    ag1_h,
    ag1_c,
    ag2_send,
    ag2_y,
    ag2_h,
    ag2_c,
    e_send,
    e_recv,
    p_send,
    p_recv,
):
    x = lax.axis_index("x")
    z = lax.axis_index("z")
    y = lax.axis_index("y")
    c = lax.axis_index("c")
    f = y * NC + c
    zp, zm = mod(z + 1, NZ), mod(z - 1, NZ)
    yp, ym, y2 = mod(y + 1, NY), mod(y - 1, NY), mod(y + 2, NY)
    oc = 1 - c
    width = out.shape[1]

    cols = pl.ds(pl.multiple_of(f * width, width), width)
    own_t = pltpu.make_async_copy(tok.at[:, cols], tbuf.at[z, :, pl.ds(0, width)], local_sem.at[0])
    own_g = pltpu.make_async_copy(grd.at[:, cols], tbuf.at[z, :, pl.ds(width, width)], local_sem.at[1])
    infos = [
        pltpu.make_async_copy(a, b, local_sem.at[5 + i])
        for i, (a, b) in enumerate(((routes_h, routes), (kept_h, kept), (probs_h, probs)))
    ]
    for copy in infos:
        copy.start()
    own_t.start()
    own_g.start()
    hid = wg.shape[1]
    loads = [
        pltpu.make_async_copy(wg, wgu.at[:, pl.ds(0, hid)], local_sem.at[2]),
        pltpu.make_async_copy(wu, wgu.at[:, pl.ds(hid, hid)], local_sem.at[3]),
        pltpu.make_async_copy(wd, wdv, local_sem.at[4]),
    ]
    for copy in loads:
        copy.start()

    barrier = pltpu.get_barrier_semaphore()
    for where in [{"z": zp}, {"z": zm}] + [{"x": mod(x + d, NX)} for d in range(1, NX)]:
        pl.semaphore_signal(barrier, inc=1, device_id=where, device_id_type=MESH)
    for d in range(1, NF):
        to = mod(f + d, NF)
        pl.semaphore_signal(
            barrier, inc=1, device_id={"y": to // NC, "c": lax.rem(to, NC)}, device_id_type=MESH
        )

    nexp = NX * NZ
    tok_rows = routes.shape[1]
    for copy in infos:
        copy.wait()
    rt = routes[...]
    e_iota = lax.broadcasted_iota(jnp.int32, (nexp, tok_rows), 0)
    named = jnp.zeros((nexp, tok_rows), F32)
    for k in range(8):
        named = named + jnp.where(rt[k : k + 1, :] == e_iota, 1.0, 0.0)
    before = lax.broadcasted_iota(jnp.int32, (tok_rows, tok_rows), 0) < lax.broadcasted_iota(
        jnp.int32, (tok_rows, tok_rows), 1
    )
    rank = jnp.dot(
        named.astype(BF16), jnp.where(before, 1.0, 0.0).astype(BF16), preferred_element_type=F32
    )
    kf = kept[...].astype(F32)
    weight = kf * probs[...]
    for k in range(8):
        slot = jnp.sum(jnp.where(rt[k : k + 1, :] == e_iota, rank, 0.0), axis=0, keepdims=True)
        dest = rt[k : k + 1, :].astype(F32) * 16.0 + slot
        rbuf[z, k : k + 1, :] = jnp.where(kf[k : k + 1, :] > 0.0, dest, -1.0)
        rbuf[z, 8 + k : 9 + k, :] = weight[k : k + 1, :]
    cst[...] = jnp.zeros_like(cst)

    pl.semaphore_wait(barrier, 2 + (NX - 1) + (NF - 1))
    own_t.wait()
    own_g.wait()

    def z_copies(direction, s, hop):
        to = zp if direction == 0 else zm
        half = tok_rows // 2
        parts = [rbuf.at[s]] + [tbuf.at[s, pl.ds(i * half, half), :] for i in range(2)]
        return [
            rdma(part, part, z_send.at[direction, min(i, 1)], z_recv.at[direction, i, hop], z=to)
            for i, part in enumerate(parts)
        ]

    def z_start(direction, s, hop):
        for copy in z_copies(direction, s, hop):
            copy.start()

    def z_pass(direction, s, hop, onward, which):
        arrived = z_copies(direction, s, hop)
        following = z_copies(direction, s, hop + 1)
        for came, goes in zip(arrived[which], following[which]):
            came.wait_recv()

            @pl.when(onward)
            def _():
                goes.start()

    z_start(0, z, 0)
    z_start(1, z, 0)

    def wblock(ref, b):
        at = pl.ds(pl.multiple_of(b * width, width), width)
        return ref.at[at, :] if ref is not wd else ref.at[:, at]

    def wplace(i, b):
        return (
            gu.at[b, :, pl.ds(0, hid)] if i == 0 else gu.at[b, :, pl.ds(hid, hid)] if i == 1 else dn.at[b]
        )

    for d in range(1, NF):
        to = mod(f + d, NF)
        for i, ref in enumerate((wg, wu, wd)):
            rdma(
                wblock(ref, to),
                wplace(i, f),
                wgt_send.at[i],
                wgt_recv.at[i, f],
                y=to // NC,
                c=lax.rem(to, NC),
            ).start()
    own_w = [
        pltpu.make_async_copy(wblock(ref, f), wplace(i, f), wgt_recv.at[i, f])
        for i, ref in enumerate((wg, wu, wd))
    ]
    for copy in own_w:
        copy.start()

    def selection(s):
        info = rbuf[s]
        r = lax.broadcasted_iota(jnp.int32, (CH, tok_rows), 0)
        name = ((r >> 4) * (NZ * 16) + (r & 15) + z * 16).astype(F32)
        hit = jnp.zeros((CH, tok_rows), F32)
        wgt = jnp.zeros((CH, tok_rows), F32)
        for k in range(8):
            same = info[k : k + 1, :] == name
            hit = hit + jnp.where(same, 1.0, 0.0)
            wgt = wgt + jnp.where(same, info[8 + k : 9 + k, :], 0.0)
        return hit, wgt

    def select_rows(s):
        hit, wgt = selection(s)
        picked = jnp.dot(hit.astype(BF16), tbuf[s], preferred_element_type=F32)
        scale = jnp.sum(wgt, axis=1, keepdims=True)
        stg[s, :, 0:width] = picked[:, :width].astype(BF16)
        stg[s, :, width:] = (picked[:, width:] * scale).astype(BF16)
        cst[...] += hit
        high = wgt.astype(BF16).astype(F32)
        turned = jnp.transpose(jnp.concatenate([high, wgt - high, hit, hit], axis=0))
        pick_o[s] = turned[:, : 2 * CH].astype(BF16)
        pick_d[s] = turned[:, 2 * CH : 3 * CH].astype(BF16)

    def x_copies(src, dst, send, recv, s):
        def part(v):
            return pl.ds(pl.multiple_of(v * 16, 16), 16)

        mine = pltpu.make_async_copy(src(s, x), dst(s, x), recv.at[s, x])
        others = []
        for d in range(1, NX):
            to = mod(x + d, NX)
            others.append(rdma(src(s, to), dst(s, x), send, recv.at[s, x], x=to))
        return mine, others

    def x_waits(src, dst, send, recv, s):
        pltpu.make_async_copy(src(s, x), dst(s, x), recv.at[s, x]).wait()
        for d in range(1, NX):
            frm = mod(x + d, NX)
            rdma(src(s, frm), dst(s, frm), send, recv.at[s, frm], x=frm).wait_recv()

    def stg_src(s, v):
        return stg.at[s, pl.ds(pl.multiple_of(v * 16, 16), 16), :]

    def xc_dst(s, v):
        return xc.at[f, pl.ds(pl.multiple_of(s * CH + v * 16, 16), 16), :]

    def x_send_rows(s):
        mine, others = x_copies(stg_src, xc_dst, x_send, x_recv, s)
        mine.start()
        for copy in others:
            copy.start()

    def x_wait_rows(s):
        x_waits(stg_src, xc_dst, x_send, x_recv, s)

    def gatherer(buf, send, ysem, hsem, csem):
        def own(s):
            here = buf.at[f, rows_of(s)]
            rdma(here, here, send.at[0], ysem.at[0, s], y=yp).start()
            rdma(here, here, send.at[1], ysem.at[1, s], y=ym).start()
            rdma(here, here, send.at[2], csem.at[0, s], c=oc).start()

        def forward(s):
            for i, (frm, to, off) in enumerate(((ym, yp, 0), (yp, ym, CH // 2))):
                b = frm * NC + c
                whole = buf.at[b, rows_of(s)]
                half = buf.at[b, rows_of(s, off, CH // 2)]
                rdma(whole, whole, send.at[i], ysem.at[i, s], y=frm).wait_recv()
                rdma(half, half, send.at[3 + i], hsem.at[i, s], y=to).start()
                rdma(whole, whole, send.at[5 + i], csem.at[1 + i, s], c=oc).start()

        def halves(s):
            b = y2 * NC + c
            whole = buf.at[b, rows_of(s)]
            for i, frm in enumerate((ym, yp)):
                half = buf.at[b, rows_of(s, i * (CH // 2), CH // 2)]
                rdma(half, half, send.at[3 + i], hsem.at[i, s], y=frm).wait_recv()
            rdma(whole, whole, send.at[7], csem.at[3, s], c=oc).start()

        def other_core(s):
            for i, yy in enumerate((y, ym, yp, y2)):
                whole = buf.at[yy * NC + oc, rows_of(s)]
                rdma(whole, whole, send.at[2], csem.at[i, s], c=oc).wait_recv()

        def drain():
            full = buf.at[f]
            half = buf.at[f, pl.ds(0, NZ * CH // 2)]
            for i in range(8):
                part = half if i in (3, 4) else full
                rdma(part, part, send.at[i], ysem.at[0, 0], c=oc).wait_send()

        return own, forward, halves, other_core, drain

    own1, forward1, halves1, other1, drain1 = gatherer(xc, ag1_send, ag1_y, ag1_h, ag1_c)
    own2, forward2, halves2, other2, drain2 = gatherer(hdu, ag2_send, ag2_y, ag2_h, ag2_c)

    for copy in loads:
        copy.wait()
    for b in range(NF):
        at = slice(b * width, (b + 1) * width)
        wdt[at, :] = jnp.transpose(wdv[:, at].astype(F32)).astype(BF16)

    def up_chunks(sa, sb):
        gate_up = jnp.zeros((2 * CH, 2 * hid), F32)
        d_hid = jnp.zeros((2 * CH, hid), F32)
        for b in range(NF):
            xs = jnp.concatenate([xc[b, rows_of(s), 0:width] for s in (sa, sb)], axis=0)
            cs = jnp.concatenate([xc[b, rows_of(s), width : 2 * width] for s in (sa, sb)], axis=0)
            gate_up += jnp.dot(xs, wgu[b * width : (b + 1) * width, :], preferred_element_type=F32)
            d_hid += jnp.dot(cs, wdt[b * width : (b + 1) * width, :], preferred_element_type=F32)
        gate, up = gate_up[:, :hid], gate_up[:, hid:]
        sig = jax.nn.sigmoid(gate)
        act = gate * sig
        slope = sig * (1.0 + gate * (1.0 - sig))
        hidden = (act * up).astype(BF16)
        d_gate = (d_hid * up * slope).astype(BF16)
        d_up = (d_hid * act).astype(BF16)
        for i, s in enumerate((sa, sb)):
            part = slice(i * CH, (i + 1) * CH)
            hdu[f, rows_of(s), 0:hid] = hidden[part]
            hdu[f, rows_of(s), hid : 2 * hid] = d_gate[part]
            hdu[f, rows_of(s), 2 * hid : 3 * hid] = d_up[part]

    def pair(k):
        return mod(z - k, NZ), mod(z + 1 + k, NZ)

    half_ring = NZ // 2

    def weights_wait():
        for copy in own_w:
            copy.wait()
        for d in range(1, NF):
            frm = mod(f + d, NF)
            for i, ref in enumerate((wg, wu, wd)):
                rdma(
                    wblock(ref, frm),
                    wplace(i, frm),
                    wgt_send.at[i],
                    wgt_recv.at[i, frm],
                    y=frm // NC,
                    c=lax.rem(frm, NC),
                ).wait_recv()

    def turn(b):
        gut[b] = jnp.transpose(gu[b].astype(F32)).astype(BF16)

    def step1(i, carry):
        sa, sb = pair(i)
        onward = i <= half_ring - 2

        def z_step(which):
            @pl.when(i < half_ring)
            def _():
                @pl.when(i >= 1)
                def _():
                    z_pass(0, sa, i - 1, onward, which)

                z_pass(1, sb, i, onward, which)

        z_step(slice(0, 2))

        @pl.when((i >= 1) & (i < half_ring + 1))
        def _():
            for s in pair(i - 1):
                x_wait_rows(s)
                own1(s)

        @pl.when((i >= 2) & (i < half_ring + 2))
        def _():
            for s in pair(i - 2):
                forward1(s)

        z_step(slice(2, 3))

        @pl.when(i < half_ring)
        def _():
            select_rows(sa)
            select_rows(sb)
            x_send_rows(sa)
            x_send_rows(sb)

        @pl.when((i >= 3) & (i < half_ring + 3))
        def _():
            for s in pair(i - 3):
                halves1(s)

        @pl.when(i == half_ring)
        def _():
            weights_wait()

        @pl.when(i >= half_ring)
        def _():
            for j in range(2):
                turn((i - half_ring) * 2 + j)

        @pl.when(i >= 4)
        def _():
            pa, pb = pair(i - 4)
            other1(pa)
            other1(pb)
            up_chunks(pa, pb)

            @pl.when(i >= half_ring + LAG - EARLY)
            def _():
                own2(pa)
                own2(pb)

        return carry

    lax.fori_loop(0, half_ring + LAG, step1, 0)

    def cst_src(s, v):
        return cst.at[pl.ds(pl.multiple_of(v * 16, 16), 16), :]

    def cst_dst(s, v):
        return crecv.at[v]

    c_mine, c_others = x_copies(cst_src, cst_dst, c_send, c_recv, 0)
    c_mine.start()
    for copy in c_others:
        copy.start()

    def count_rows():
        x_waits(cst_src, cst_dst, c_send, c_recv, 0)
        total = jnp.sum(jnp.sum(crecv[...], axis=0), axis=0, keepdims=True)
        count = jnp.sum(total, axis=1, keepdims=True)
        inv_ref[...] = jnp.broadcast_to(1.0 / jnp.maximum(count, 1.0), inv_ref.shape)

    def back_pair(m):
        return mod(z + half_ring - m, NZ), mod(z - (half_ring - 1) + m, NZ)

    def down_chunks(sa, sb):
        e_out = jnp.zeros((2 * CH, width), F32)
        d_row = jnp.zeros((2 * CH, width), F32)
        for b in range(NF):
            hs = jnp.concatenate([hdu[b, rows_of(s), 0:hid] for s in (sa, sb)], axis=0)
            ds = jnp.concatenate([hdu[b, rows_of(s), hid : 3 * hid] for s in (sa, sb)], axis=0)
            e_out += jnp.dot(hs, dn[b], preferred_element_type=F32)
            d_row += jnp.dot(ds, gut[b], preferred_element_type=F32)
        for i, s in enumerate((sa, sb)):
            part = slice(i * CH, (i + 1) * CH)
            eo[s, :, 0:width] = e_out[part].astype(BF16)
            eo[s, :, width:] = d_row[part].astype(BF16)

    def eo_src(s, v):
        return eo.at[s, pl.ds(pl.multiple_of(v * 16, 16), 16), :]

    def ret_dst(s, v):
        return ret.at[s, pl.ds(pl.multiple_of(v * 16, 16), 16), :]

    def share(kind, s):
        if kind == 1:
            return jnp.dot(pick_d[s], ret[s, :, width:], preferred_element_type=F32)
        back = ret[s, :, 0:width]
        return jnp.dot(
            pick_o[s], jnp.concatenate([back, back], axis=0), preferred_element_type=F32
        )

    def p_copy(direction, kind, m):
        to = zp if direction == 0 else zm
        return rdma(
            psend.at[direction, m, kind],
            precv.at[direction, m, kind],
            p_send.at[direction],
            p_recv.at[direction, m, kind],
            z=to,
        )

    def pass_on(direction, kind, s, m):
        part = share(kind, s)

        @pl.when(m == 0)
        def _():
            psend[direction, m, kind] = part.astype(BF16)

        @pl.when(m >= 1)
        def _():
            before_m = jnp.maximum(m - 1, 0)
            p_copy(direction, kind, before_m).wait_recv()
            came = precv[direction, before_m, kind].astype(F32)
            psend[direction, m, kind] = (part + came).astype(BF16)

        p_copy(direction, kind, m).start()

    def grad_out(b):
        at = pl.ds(pl.multiple_of(b * width, width), width)
        return [
            pltpu.make_async_copy(gg.at[at, pl.ds(0, hid)], ggate.at[at, :], grad_sem.at[0]),
            pltpu.make_async_copy(gg.at[at, pl.ds(hid, hid)], gup.at[at, :], grad_sem.at[1]),
            pltpu.make_async_copy(gdn.at[:, at], gdown.at[:, at], grad_sem.at[2]),
        ]

    def grads(b):
        at = pl.ds(pl.multiple_of(b * width, width), width)
        inv = inv_ref[0:1, 0:1]
        d_gu = lax.dot_general(
            xc[b, :, 0:width], hdu[f, :, hid : 3 * hid], TN, preferred_element_type=F32
        )
        gg[at, :] = (d_gu * inv).astype(BF16)
        d_dn = lax.dot_general(
            hdu[f, :, 0:hid], xc[b, :, width : 2 * width], TN, preferred_element_type=F32
        )
        gdn[:, at] = (d_dn * inv).astype(BF16)

    def step2(i, carry):
        def pass_kind(kind):
            @pl.when(i >= 3)
            def _():
                m = i - 3
                chunks = back_pair(m)
                if kind == 0:
                    for s in chunks:
                        x_waits(eo_src, ret_dst, e_send, e_recv, s)
                for direction in range(2):
                    pass_on(direction, kind, chunks[direction], m)

        @pl.when(i < half_ring - EARLY)
        def _():
            for s in back_pair(i + EARLY):
                own2(s)

        pass_kind(0)

        @pl.when(i < half_ring)
        def _():
            for s in back_pair(i):
                forward2(s)

        @pl.when(i >= 2)
        def _():
            chunks = back_pair(i - 2)
            for s in chunks:
                other2(s)
            down_chunks(*chunks)
            for s in chunks:
                mine, others = x_copies(eo_src, ret_dst, e_send, e_recv, s)
                mine.start()
                for copy in others:
                    copy.start()

        @pl.when((i >= 1) & (i < half_ring + 1))
        def _():
            for s in back_pair(i - 1):
                halves2(s)

        pass_kind(1)

        @pl.when(i == 0)
        def _():
            count_rows()

        @pl.when((i >= 1) & (i < half_ring + 1))
        def _():
            for copy in grad_out(i - 1):
                copy.start()

        @pl.when(i < half_ring)
        def _():
            grads(i)

        return carry

    lax.fori_loop(0, half_ring + 2, step2, 0)

    last = half_ring - 1
    sa, sb = back_pair(last)
    x_waits(eo_src, ret_dst, e_send, e_recv, sa)
    for kind in range(2):
        pass_on(0, kind, sa, jnp.int32(last))
    x_waits(eo_src, ret_dst, e_send, e_recv, sb)
    for kind, ref in enumerate((out, ing)):
        part = share(kind, sb)
        p_copy(1, kind, last - 1).wait_recv()
        part += precv[1, last - 1, kind].astype(F32)
        p_copy(0, kind, last).wait_recv()
        ref[...] = (part + precv[0, last, kind].astype(F32)).astype(BF16)

    drain1()
    drain2()
    for direction, hops in ((0, half_ring - 1), (1, half_ring)):
        to = zp if direction == 0 else zm
        for i, buf in enumerate((rbuf, tbuf)):
            part = buf.at[pl.ds(0, hops)]
            rdma(part, part, z_send.at[direction, i], z_recv.at[direction, i, 0], z=to).wait_send()
    x_part = NZ * (NX - 1) // NX
    for ref, sem in ((stg, x_send), (eo, e_send)):
        part = ref.at[pl.ds(0, x_part)]
        rdma(part, part, sem, x_recv.at[0, 0], x=mod(x + 1, NX)).wait_send()
    part = crecv.at[pl.ds(0, NX - 1)]
    rdma(part, part, c_send, c_recv.at[0, 0], x=mod(x + 1, NX)).wait_send()
    for direction, hops in ((0, half_ring), (1, half_ring - 1)):
        part = psend.at[direction, pl.ds(0, hops)]
        to = zp if direction == 0 else zm
        rdma(part, part, p_send.at[direction], p_recv.at[direction, 0], z=to).wait_send()
    for i, ref in enumerate((wg, wu, wd)):
        at = pl.ds(0, (NF - 1) * width)
        part = ref.at[at, :] if i < 2 else ref.at[:, at]
        rdma(part, part, wgt_send.at[i], wgt_recv.at[i, 0], c=oc).wait_send()
    pltpu.make_async_copy(gg.at[:, pl.ds(0, hid)], ggate, grad_sem.at[0]).wait()
    pltpu.make_async_copy(gg.at[:, pl.ds(hid, hid)], gup, grad_sem.at[1]).wait()
    pltpu.make_async_copy(gdn, gdown, grad_sem.at[2]).wait()


def put_out(n, *refs):
    srcs, dsts, bufs, sems = refs[:n], refs[n : 2 * n], refs[2 * n : 3 * n], refs[3 * n]
    ins = [pltpu.make_async_copy(srcs[i], bufs[i], sems.at[0, i]) for i in range(n)]
    outs = [pltpu.make_async_copy(bufs[i], dsts[i], sems.at[1, i]) for i in range(n)]
    for copy in ins:
        copy.start()
    for came, goes in zip(ins, outs):
        came.wait()
        goes.start()
    for copy in outs:
        copy.wait()


def per_device(tokens, routes, kept_mask, gate_probs, output_grad, w_gate, w_up, w_down):
    tok_rows, model = tokens.shape
    width = model // NF
    hid = w_gate.shape[2]
    wg, wu, wd = w_gate[0], w_up[0], w_down[0]
    vmem = pl.BlockSpec(memory_space=pltpu.VMEM)
    hbm = pl.BlockSpec(memory_space=pl.ANY)
    src = pl.BlockSpec(memory_space=pltpu.HBM)
    dma = pltpu.SemaphoreType.DMA
    gather_sems = [dma((8,)), dma((2, NZ)), dma((2, NZ)), dma((4, NZ))]
    outs = pl.pallas_call(
        kernel,
        out_shape=(
            jax.ShapeDtypeStruct((tok_rows, width), BF16),
            jax.ShapeDtypeStruct((tok_rows, width), BF16),
            jax.ShapeDtypeStruct(wg.shape, BF16),
            jax.ShapeDtypeStruct(wu.shape, BF16),
            jax.ShapeDtypeStruct(wd.shape, BF16),
        ),
        in_specs=[src] * 8,
        out_specs=[vmem] * 2 + [hbm] * 3,
        scratch_shapes=[
            pltpu.VMEM((NZ, tok_rows, 2 * width), BF16),
            pltpu.VMEM((NZ, 16, tok_rows), F32),
            pltpu.VMEM((NZ, CH, 2 * width), BF16),
            pltpu.VMEM((NF, NZ * CH, 2 * width), BF16),
            pltpu.VMEM((NF, NZ * CH, 3 * hid), BF16),
            pltpu.VMEM((model, 2 * hid), BF16),
            pltpu.VMEM((NF, width, 2 * hid), BF16),
            pltpu.VMEM((NF, hid, width), BF16),
            pltpu.VMEM((NZ, CH, 2 * width), BF16),
            pltpu.VMEM((NZ, CH, 2 * width), BF16),
            pltpu.VMEM((2, NZ // 2, 2, tok_rows, width), BF16),
            pltpu.VMEM((2, NZ // 2, 2, tok_rows, width), BF16),
            pltpu.VMEM((CH, tok_rows), F32),
            pltpu.VMEM((NX, 16, tok_rows), F32),
            pltpu.VMEM((hid, model), BF16),
            pltpu.VMEM((model, 2 * hid), BF16),
            pltpu.VMEM((hid, model), BF16),
            pltpu.VMEM((8, 128), F32),
            pltpu.VMEM((NZ, tok_rows, 2 * CH), BF16),
            pltpu.VMEM((NZ, tok_rows, CH), BF16),
            pltpu.VMEM((model, hid), BF16),
            pltpu.VMEM((NF, 2 * hid, width), BF16),
            pltpu.VMEM((8, tok_rows), jnp.int32),
            pltpu.VMEM((8, tok_rows), jnp.int32),
            pltpu.VMEM((8, tok_rows), F32),
            dma((8,)),
            dma((3,)),
            dma((3,)),
            dma((3, NF)),
            dma((2, 2)),
            dma((2, 3, NZ // 2)),
            dma(()),
            dma((NZ, NX)),
            dma(()),
            dma((1, NX)),
            *gather_sems,
            *gather_sems,
            dma(()),
            dma((NZ, NX)),
            dma((2,)),
            dma((2, NZ // 2, 2)),
        ],
        compiler_params=pltpu.CompilerParams(
            collective_id=0, has_side_effects=True, vmem_limit_bytes=58 * 1024 * 1024
        ),
    )(tokens, output_grad, routes.T, kept_mask.T, gate_probs.T, wg, wu, wd)
    output, input_grad, g_gate, g_up, g_down = pl.pallas_call(
        functools.partial(put_out, len(outs)),
        out_shape=tuple(jax.ShapeDtypeStruct(o.shape, o.dtype) for o in outs),
        in_specs=[hbm] * 5,
        out_specs=[hbm] * 5,
        scratch_shapes=[pltpu.VMEM(o.shape, o.dtype) for o in outs] + [dma((2, 5))],
        compiler_params=pltpu.CompilerParams(vmem_limit_bytes=58 * 1024 * 1024),
    )(*outs)
    return output, input_grad, g_gate[None], g_up[None], g_down[None]


def solution(mesh):
    torus = Mesh(mesh.devices.reshape(NX, NZ, NY, NC), ("x", "z", "y", "c"))
    dp, expert = ("x", "z"), ("y", "c")
    return jax.shard_map(
        per_device,
        mesh=torus,
        in_specs=(
            P(dp, None),
            P(dp, None),
            P(dp, None),
            P(dp, None),
            P(dp, None),
            P(dp, None, expert),
            P(dp, None, expert),
            P(dp, expert, None),
        ),
        out_specs=(
            P(dp, expert),
            P(dp, expert),
            P(dp, None, expert),
            P(dp, None, expert),
            P(dp, expert, None),
        ),
        check_vma=False,
    )
```

```python
import functools

import jax
import jax.numpy as jnp
from jax import lax
from jax.experimental import pallas as pl
from jax.experimental.pallas import tpu as pltpu
from jax.sharding import Mesh
from jax.sharding import PartitionSpec as P

MESH = pl.DeviceIdType.MESH
F32 = jnp.float32
BF16 = jnp.bfloat16

NX, NZ, NY, NC = 4, 16, 4, 2
NF = NY * NC
CH = 64
LAG = 4
EARLY = 1
EARLY_W = (0, 1)
LATE_W = (2,)
LATE = 10
TN = (((0,), (0,)), ((), ()))


def rdma(src, dst, send_sem, recv_sem, **where):
    return pltpu.make_async_remote_copy(
        src_ref=src,
        dst_ref=dst,
        send_sem=send_sem,
        recv_sem=recv_sem,
        device_id=where,
        device_id_type=MESH,
    )


def rows_of(s, off=0, size=CH):
    return pl.ds(pl.multiple_of(s * CH + off, 16), size)


def mod(v, n):
    return lax.rem(v + 2 * n, n)


def kernel(
    tok,
    grd,
    routes_h,
    kept_h,
    probs_h,
    wg,
    wu,
    wd,
    out,
    ing,
    ggate,
    gup,
    gdown,
    tbuf,
    rbuf,
    stg,
    xc,
    hdu,
    wgu,
    gu,
    dn,
    eo,
    ret,
    psend,
    precv,
    cst,
    crecv,
    wdv,
    gg,
    gdn,
    inv_ref,
    pick_o,
    pick_d,
    wdt,
    gut,
    routes,
    kept,
    probs,
    local_sem,
    grad_sem,
    wgt_send,
    wgt_recv,
    z_send,
    z_recv,
    x_send,
    x_recv,
    c_send,
    c_recv,
    ag1_send,
    ag1_y,
    ag1_h,
    ag1_c,
    ag2_send,
    ag2_y,
    ag2_h,
    ag2_c,
    e_send,
    e_recv,
    p_send,
    p_recv,
):
    x = lax.axis_index("x")
    z = lax.axis_index("z")
    y = lax.axis_index("y")
    c = lax.axis_index("c")
    f = y * NC + c
    zp, zm = mod(z + 1, NZ), mod(z - 1, NZ)
    yp, ym, y2 = mod(y + 1, NY), mod(y - 1, NY), mod(y + 2, NY)
    oc = 1 - c
    width = out.shape[1]
    tok_rows = routes.shape[1]

    cols = pl.ds(pl.multiple_of(f * width, width), width)
    own_t = pltpu.make_async_copy(tok.at[:, cols], tbuf.at[z, :, pl.ds(0, width)], local_sem.at[0])
    own_g = pltpu.make_async_copy(grd.at[:, cols], tbuf.at[z, :, pl.ds(width, width)], local_sem.at[1])
    infos = [
        pltpu.make_async_copy(a, b, local_sem.at[5 + i])
        for i, (a, b) in enumerate(((routes_h, routes), (kept_h, kept), (probs_h, probs)))
    ]
    for copy in infos:
        copy.start()
    own_t.start()
    own_g.start()
    hid = wg.shape[1]
    loads = [
        pltpu.make_async_copy(wg, wgu.at[:, pl.ds(0, hid)], local_sem.at[2]),
        pltpu.make_async_copy(wu, wgu.at[:, pl.ds(hid, hid)], local_sem.at[3]),
        pltpu.make_async_copy(wd, wdv, local_sem.at[4]),
    ]
    for copy in loads:
        copy.start()

    barrier = pltpu.get_barrier_semaphore()
    for where in [{"z": zp}, {"z": zm}] + [{"x": mod(x + d, NX)} for d in range(1, NX)]:
        pl.semaphore_signal(barrier, inc=1, device_id=where, device_id_type=MESH)
    for d in range(1, NF):
        to = mod(f + d, NF)
        pl.semaphore_signal(
            barrier, inc=1, device_id={"y": to // NC, "c": lax.rem(to, NC)}, device_id_type=MESH
        )

    pl.semaphore_wait(barrier, 2 + (NX - 1) + (NF - 1))
    own_t.wait()
    own_g.wait()

    def z_copies(direction, s, hop):
        to = zp if direction == 0 else zm
        half = tok_rows // 2
        parts = [rbuf.at[s]] + [tbuf.at[s, pl.ds(i * half, half), :] for i in range(2)]
        return [
            rdma(part, part, z_send.at[direction, min(i, 1)], z_recv.at[direction, i, hop], z=to)
            for i, part in enumerate(parts)
        ]

    def z_pass(direction, s, hop, onward, which):
        arrived = z_copies(direction, s, hop)
        following = z_copies(direction, s, hop + 1)
        for came, goes in zip(arrived[which], following[which]):
            came.wait_recv()

            @pl.when(onward)
            def _():
                goes.start()

    for direction in range(2):
        for copy in z_copies(direction, z, 0)[1:]:
            copy.start()

    def wblock(ref, b):
        at = pl.ds(pl.multiple_of(b * width, width), width)
        return ref.at[at, :] if ref is not wd else ref.at[:, at]

    def wplace(i, b):
        return (
            gu.at[b, :, pl.ds(0, hid)] if i == 0 else gu.at[b, :, pl.ds(hid, hid)] if i == 1 else dn.at[b]
        )

    def weights_send(d, kinds):
        to = mod(f + d, NF)
        for i in kinds:
            ref = (wg, wu, wd)[i]
            rdma(
                wblock(ref, to),
                wplace(i, f),
                wgt_send.at[i],
                wgt_recv.at[i, f],
                y=to // NC,
                c=lax.rem(to, NC),
            ).start()

    for d in range(1, NF):
        weights_send(d, EARLY_W)
    own_w = [
        pltpu.make_async_copy(wblock(ref, f), wplace(i, f), wgt_recv.at[i, f])
        for i, ref in enumerate((wg, wu, wd))
    ]
    for copy in own_w:
        copy.start()

    nexp = NX * NZ
    for copy in infos:
        copy.wait()
    rt = routes[...]
    e_iota = lax.broadcasted_iota(jnp.int32, (nexp, tok_rows), 0)
    named = jnp.zeros((nexp, tok_rows), F32)
    for k in range(8):
        named = named + jnp.where(rt[k : k + 1, :] == e_iota, 1.0, 0.0)
    before = lax.broadcasted_iota(jnp.int32, (tok_rows, tok_rows), 0) < lax.broadcasted_iota(
        jnp.int32, (tok_rows, tok_rows), 1
    )
    rank = jnp.dot(
        named.astype(BF16), jnp.where(before, 1.0, 0.0).astype(BF16), preferred_element_type=F32
    )
    kf = kept[...].astype(F32)
    weight = kf * probs[...]
    for k in range(8):
        slot = jnp.sum(jnp.where(rt[k : k + 1, :] == e_iota, rank, 0.0), axis=0, keepdims=True)
        dest = rt[k : k + 1, :].astype(F32) * 16.0 + slot
        rbuf[z, k : k + 1, :] = jnp.where(kf[k : k + 1, :] > 0.0, dest, -1.0)
        rbuf[z, 8 + k : 9 + k, :] = weight[k : k + 1, :]
    cst[...] = jnp.zeros_like(cst)

    for direction in range(2):
        z_copies(direction, z, 0)[0].start()

    def selection(s):
        info = rbuf[s]
        r = lax.broadcasted_iota(jnp.int32, (CH, tok_rows), 0)
        name = ((r >> 4) * (NZ * 16) + (r & 15) + z * 16).astype(F32)
        hit = jnp.zeros((CH, tok_rows), F32)
        wgt = jnp.zeros((CH, tok_rows), F32)
        for k in range(8):
            same = info[k : k + 1, :] == name
            hit = hit + jnp.where(same, 1.0, 0.0)
            wgt = wgt + jnp.where(same, info[8 + k : 9 + k, :], 0.0)
        return hit, wgt

    def select_rows(s):
        hit, wgt = selection(s)
        picked = jnp.dot(hit.astype(BF16), tbuf[s], preferred_element_type=F32)
        scale = jnp.sum(wgt, axis=1, keepdims=True)
        stg[s, :, 0:width] = picked[:, :width].astype(BF16)
        stg[s, :, width:] = (picked[:, width:] * scale).astype(BF16)
        cst[...] += hit
        high = wgt.astype(BF16).astype(F32)
        turned = jnp.transpose(jnp.concatenate([high, wgt - high, hit, hit], axis=0))
        pick_o[s] = turned[:, : 2 * CH].astype(BF16)
        pick_d[s] = turned[:, 2 * CH : 3 * CH].astype(BF16)

    def x_copies(src, dst, send, recv, s):
        def part(v):
            return pl.ds(pl.multiple_of(v * 16, 16), 16)

        mine = pltpu.make_async_copy(src(s, x), dst(s, x), recv.at[s, x])
        others = []
        for d in range(1, NX):
            to = mod(x + d, NX)
            others.append(rdma(src(s, to), dst(s, x), send, recv.at[s, x], x=to))
        return mine, others

    def x_waits(src, dst, send, recv, s):
        pltpu.make_async_copy(src(s, x), dst(s, x), recv.at[s, x]).wait()
        for d in range(1, NX):
            frm = mod(x + d, NX)
            rdma(src(s, frm), dst(s, frm), send, recv.at[s, frm], x=frm).wait_recv()

    def stg_src(s, v):
        return stg.at[s, pl.ds(pl.multiple_of(v * 16, 16), 16), :]

    def xc_dst(s, v):
        return xc.at[f, pl.ds(pl.multiple_of(s * CH + v * 16, 16), 16), :]

    def x_send_rows(s):
        mine, others = x_copies(stg_src, xc_dst, x_send, x_recv, s)
        mine.start()
        for copy in others:
            copy.start()

    def x_wait_rows(s):
        x_waits(stg_src, xc_dst, x_send, x_recv, s)

    def gatherer(buf, send, ysem, hsem, csem):
        def own(s):
            here = buf.at[f, rows_of(s)]
            rdma(here, here, send.at[0], ysem.at[0, s], y=yp).start()
            rdma(here, here, send.at[1], ysem.at[1, s], y=ym).start()
            rdma(here, here, send.at[2], csem.at[0, s], c=oc).start()

        def forward(s):
            for i, (frm, to, off) in enumerate(((ym, yp, 0), (yp, ym, CH // 2))):
                b = frm * NC + c
                whole = buf.at[b, rows_of(s)]
                half = buf.at[b, rows_of(s, off, CH // 2)]
                rdma(whole, whole, send.at[i], ysem.at[i, s], y=frm).wait_recv()
                rdma(half, half, send.at[3 + i], hsem.at[i, s], y=to).start()
                rdma(whole, whole, send.at[5 + i], csem.at[1 + i, s], c=oc).start()

        def halves(s):
            b = y2 * NC + c
            whole = buf.at[b, rows_of(s)]
            for i, frm in enumerate((ym, yp)):
                half = buf.at[b, rows_of(s, i * (CH // 2), CH // 2)]
                rdma(half, half, send.at[3 + i], hsem.at[i, s], y=frm).wait_recv()
            rdma(whole, whole, send.at[7], csem.at[3, s], c=oc).start()

        def other_core(s):
            for i, yy in enumerate((y, ym, yp, y2)):
                whole = buf.at[yy * NC + oc, rows_of(s)]
                rdma(whole, whole, send.at[2], csem.at[i, s], c=oc).wait_recv()

        def drain():
            full = buf.at[f]
            half = buf.at[f, pl.ds(0, NZ * CH // 2)]
            for i in range(8):
                part = half if i in (3, 4) else full
                rdma(part, part, send.at[i], ysem.at[0, 0], c=oc).wait_send()

        return own, forward, halves, other_core, drain

    own1, forward1, halves1, other1, drain1 = gatherer(xc, ag1_send, ag1_y, ag1_h, ag1_c)
    own2, forward2, halves2, other2, drain2 = gatherer(hdu, ag2_send, ag2_y, ag2_h, ag2_c)

    for copy in loads:
        copy.wait()
    for b in range(NF):
        at = slice(b * width, (b + 1) * width)
        wdt[at, :] = jnp.transpose(wdv[:, at].astype(F32)).astype(BF16)

    def up_chunks(sa, sb):
        gate_up = jnp.zeros((2 * CH, 2 * hid), F32)
        d_hid = jnp.zeros((2 * CH, hid), F32)
        for b in range(NF):
            xs = jnp.concatenate([xc[b, rows_of(s), 0:width] for s in (sa, sb)], axis=0)
            cs = jnp.concatenate([xc[b, rows_of(s), width : 2 * width] for s in (sa, sb)], axis=0)
            gate_up += jnp.dot(xs, wgu[b * width : (b + 1) * width, :], preferred_element_type=F32)
            d_hid += jnp.dot(cs, wdt[b * width : (b + 1) * width, :], preferred_element_type=F32)
        gate, up = gate_up[:, :hid], gate_up[:, hid:]
        sig = jax.nn.sigmoid(gate)
        act = gate * sig
        slope = sig * (1.0 + gate * (1.0 - sig))
        hidden = (act * up).astype(BF16)
        d_gate = (d_hid * up * slope).astype(BF16)
        d_up = (d_hid * act).astype(BF16)
        for i, s in enumerate((sa, sb)):
            part = slice(i * CH, (i + 1) * CH)
            hdu[f, rows_of(s), 0:hid] = hidden[part]
            hdu[f, rows_of(s), hid : 2 * hid] = d_gate[part]
            hdu[f, rows_of(s), 2 * hid : 3 * hid] = d_up[part]

    def pair(k):
        return mod(z - k, NZ), mod(z + 1 + k, NZ)

    half_ring = NZ // 2

    def weights_wait(kinds):
        for i in kinds:
            own_w[i].wait()
        for d in range(1, NF):
            frm = mod(f + d, NF)
            for i in kinds:
                ref = (wg, wu, wd)[i]
                rdma(
                    wblock(ref, frm),
                    wplace(i, frm),
                    wgt_send.at[i],
                    wgt_recv.at[i, frm],
                    y=frm // NC,
                    c=lax.rem(frm, NC),
                ).wait_recv()

    def turn(b):
        gut[b] = jnp.transpose(gu[b].astype(F32)).astype(BF16)

    def step1(i, carry):
        sa, sb = pair(i)
        onward = i <= half_ring - 2

        def z_step(which):
            @pl.when(i < half_ring)
            def _():
                @pl.when(i >= 1)
                def _():
                    z_pass(0, sa, i - 1, onward, which)

                z_pass(1, sb, i, onward, which)

        z_step(slice(0, 2))

        @pl.when((i >= 1) & (i < half_ring + 1))
        def _():
            for s in pair(i - 1):
                x_wait_rows(s)
                own1(s)

        @pl.when((i >= 2) & (i < half_ring + 2))
        def _():
            for s in pair(i - 2):
                forward1(s)

        z_step(slice(2, 3))

        @pl.when(i == LATE)
        def _():
            for d in range(1, NF):
                weights_send(d, LATE_W)

        @pl.when(i < half_ring)
        def _():
            select_rows(sa)
            select_rows(sb)
            x_send_rows(sa)
            x_send_rows(sb)

        @pl.when((i >= 3) & (i < half_ring + 3))
        def _():
            for s in pair(i - 3):
                halves1(s)

        @pl.when(i == half_ring)
        def _():
            weights_wait(EARLY_W)

        @pl.when(i >= half_ring)
        def _():
            for j in range(2):
                turn((i - half_ring) * 2 + j)

        @pl.when(i >= 4)
        def _():
            pa, pb = pair(i - 4)
            other1(pa)
            other1(pb)
            up_chunks(pa, pb)

            @pl.when(i >= half_ring + LAG - EARLY)
            def _():
                own2(pa)
                own2(pb)

        return carry

    lax.fori_loop(0, half_ring + LAG, step1, 0)

    def cst_src(s, v):
        return cst.at[pl.ds(pl.multiple_of(v * 16, 16), 16), :]

    def cst_dst(s, v):
        return crecv.at[v]

    c_mine, c_others = x_copies(cst_src, cst_dst, c_send, c_recv, 0)
    c_mine.start()
    for copy in c_others:
        copy.start()

    def count_rows():
        x_waits(cst_src, cst_dst, c_send, c_recv, 0)
        total = jnp.sum(jnp.sum(crecv[...], axis=0), axis=0, keepdims=True)
        count = jnp.sum(total, axis=1, keepdims=True)
        inv_ref[...] = jnp.broadcast_to(1.0 / jnp.maximum(count, 1.0), inv_ref.shape)

    def back_pair(m):
        return mod(z + half_ring - m, NZ), mod(z - (half_ring - 1) + m, NZ)

    def down_chunks(sa, sb):
        e_out = jnp.zeros((2 * CH, width), F32)
        d_row = jnp.zeros((2 * CH, width), F32)
        for b in range(NF):
            hs = jnp.concatenate([hdu[b, rows_of(s), 0:hid] for s in (sa, sb)], axis=0)
            ds = jnp.concatenate([hdu[b, rows_of(s), hid : 3 * hid] for s in (sa, sb)], axis=0)
            e_out += jnp.dot(hs, dn[b], preferred_element_type=F32)
            d_row += jnp.dot(ds, gut[b], preferred_element_type=F32)
        for i, s in enumerate((sa, sb)):
            part = slice(i * CH, (i + 1) * CH)
            eo[s, :, 0:width] = e_out[part].astype(BF16)
            eo[s, :, width:] = d_row[part].astype(BF16)

    def eo_src(s, v):
        return eo.at[s, pl.ds(pl.multiple_of(v * 16, 16), 16), :]

    def ret_dst(s, v):
        return ret.at[s, pl.ds(pl.multiple_of(v * 16, 16), 16), :]

    def share(kind, s):
        if kind == 1:
            return jnp.dot(pick_d[s], ret[s, :, width:], preferred_element_type=F32)
        back = ret[s, :, 0:width]
        return jnp.dot(
            pick_o[s], jnp.concatenate([back, back], axis=0), preferred_element_type=F32
        )

    halves = [pl.ds(i * (tok_rows // 2), tok_rows // 2) for i in range(2)]

    def p_copy(direction, kind, m, h):
        to = zp if direction == 0 else zm
        return rdma(
            psend.at[direction, m, kind, halves[h], :],
            precv.at[direction, m, kind, halves[h], :],
            p_send.at[direction],
            p_recv.at[direction, m, 2 * kind + h],
            z=to,
        )

    def pass_on(direction, kind, s, m):
        part = share(kind, s)
        for h in range(2):
            mine = part[h * (tok_rows // 2) : (h + 1) * (tok_rows // 2)]

            @pl.when(m == 0)
            def _():
                psend[direction, m, kind, halves[h], :] = mine.astype(BF16)

            @pl.when(m >= 1)
            def _():
                before_m = jnp.maximum(m - 1, 0)
                p_copy(direction, kind, before_m, h).wait_recv()
                came = precv[direction, before_m, kind, halves[h], :].astype(F32)
                psend[direction, m, kind, halves[h], :] = (mine + came).astype(BF16)

            p_copy(direction, kind, m, h).start()

    def grad_out(b):
        at = pl.ds(pl.multiple_of(b * width, width), width)
        return [
            pltpu.make_async_copy(gg.at[at, pl.ds(0, hid)], ggate.at[at, :], grad_sem.at[0]),
            pltpu.make_async_copy(gg.at[at, pl.ds(hid, hid)], gup.at[at, :], grad_sem.at[1]),
            pltpu.make_async_copy(gdn.at[:, at], gdown.at[:, at], grad_sem.at[2]),
        ]

    def grads(b):
        at = pl.ds(pl.multiple_of(b * width, width), width)
        inv = inv_ref[0:1, 0:1]
        d_gu = lax.dot_general(
            xc[b, :, 0:width], hdu[f, :, hid : 3 * hid], TN, preferred_element_type=F32
        )
        gg[at, :] = (d_gu * inv).astype(BF16)
        d_dn = lax.dot_general(
            hdu[f, :, 0:hid], xc[b, :, width : 2 * width], TN, preferred_element_type=F32
        )
        gdn[:, at] = (d_dn * inv).astype(BF16)

    def step2(i, carry):
        def pass_kind(kind):
            @pl.when(i >= 3)
            def _():
                m = i - 3
                chunks = back_pair(m)
                if kind == 0:
                    for s in chunks:
                        x_waits(eo_src, ret_dst, e_send, e_recv, s)
                for direction in range(2):
                    pass_on(direction, kind, chunks[direction], m)

        @pl.when(i < half_ring - EARLY)
        def _():
            for s in back_pair(i + EARLY):
                own2(s)

        pass_kind(0)

        @pl.when(i < half_ring)
        def _():
            for s in back_pair(i):
                forward2(s)

        @pl.when(i == 2)
        def _():
            weights_wait(LATE_W)

        @pl.when(i >= 2)
        def _():
            chunks = back_pair(i - 2)
            for s in chunks:
                other2(s)
            down_chunks(*chunks)
            for s in chunks:
                mine, others = x_copies(eo_src, ret_dst, e_send, e_recv, s)
                mine.start()
                for copy in others:
                    copy.start()

        @pl.when((i >= 1) & (i < half_ring + 1))
        def _():
            for s in back_pair(i - 1):
                halves2(s)

        pass_kind(1)

        @pl.when(i == 0)
        def _():
            count_rows()

        @pl.when((i >= 1) & (i < half_ring + 1))
        def _():
            for copy in grad_out(i - 1):
                copy.start()

        @pl.when(i < half_ring)
        def _():
            grads(i)

        return carry

    lax.fori_loop(0, half_ring + 2, step2, 0)

    last = half_ring - 1
    sa, sb = back_pair(last)
    x_waits(eo_src, ret_dst, e_send, e_recv, sa)
    for kind in range(2):
        pass_on(0, kind, sa, jnp.int32(last))
    x_waits(eo_src, ret_dst, e_send, e_recv, sb)
    for kind, ref in enumerate((out, ing)):
        part = share(kind, sb)
        for h in range(2):
            p_copy(1, kind, last - 1, h).wait_recv()
        part += precv[1, last - 1, kind].astype(F32)
        for h in range(2):
            p_copy(0, kind, last, h).wait_recv()
        ref[...] = (part + precv[0, last, kind].astype(F32)).astype(BF16)

    drain1()
    drain2()
    for direction, hops in ((0, half_ring - 1), (1, half_ring)):
        to = zp if direction == 0 else zm
        for i, buf in enumerate((rbuf, tbuf)):
            part = buf.at[pl.ds(0, hops)]
            rdma(part, part, z_send.at[direction, i], z_recv.at[direction, i, 0], z=to).wait_send()
    x_part = NZ * (NX - 1) // NX
    for ref, sem in ((stg, x_send), (eo, e_send)):
        part = ref.at[pl.ds(0, x_part)]
        rdma(part, part, sem, x_recv.at[0, 0], x=mod(x + 1, NX)).wait_send()
    part = crecv.at[pl.ds(0, NX - 1)]
    rdma(part, part, c_send, c_recv.at[0, 0], x=mod(x + 1, NX)).wait_send()
    for direction, hops in ((0, half_ring), (1, half_ring - 1)):
        part = psend.at[direction, pl.ds(0, hops)]
        to = zp if direction == 0 else zm
        rdma(part, part, p_send.at[direction], p_recv.at[direction, 0], z=to).wait_send()
    for i, ref in enumerate((wg, wu, wd)):
        at = pl.ds(0, (NF - 1) * width)
        part = ref.at[at, :] if i < 2 else ref.at[:, at]
        rdma(part, part, wgt_send.at[i], wgt_recv.at[i, 0], c=oc).wait_send()
    pltpu.make_async_copy(gg.at[:, pl.ds(0, hid)], ggate, grad_sem.at[0]).wait()
    pltpu.make_async_copy(gg.at[:, pl.ds(hid, hid)], gup, grad_sem.at[1]).wait()
    pltpu.make_async_copy(gdn, gdown, grad_sem.at[2]).wait()


def put_out(n, *refs):
    srcs, dsts, bufs, sems = refs[:n], refs[n : 2 * n], refs[2 * n : 3 * n], refs[3 * n]
    ins = [pltpu.make_async_copy(srcs[i], bufs[i], sems.at[0, i]) for i in range(n)]
    outs = [pltpu.make_async_copy(bufs[i], dsts[i], sems.at[1, i]) for i in range(n)]
    for copy in ins:
        copy.start()
    for came, goes in zip(ins, outs):
        came.wait()
        goes.start()
    for copy in outs:
        copy.wait()


def per_device(tokens, routes, kept_mask, gate_probs, output_grad, w_gate, w_up, w_down):
    tok_rows, model = tokens.shape
    width = model // NF
    hid = w_gate.shape[2]
    wg, wu, wd = w_gate[0], w_up[0], w_down[0]
    vmem = pl.BlockSpec(memory_space=pltpu.VMEM)
    hbm = pl.BlockSpec(memory_space=pl.ANY)
    src = pl.BlockSpec(memory_space=pltpu.HBM)
    dma = pltpu.SemaphoreType.DMA
    gather_sems = [dma((8,)), dma((2, NZ)), dma((2, NZ)), dma((4, NZ))]
    outs = pl.pallas_call(
        kernel,
        out_shape=(
            jax.ShapeDtypeStruct((tok_rows, width), BF16),
            jax.ShapeDtypeStruct((tok_rows, width), BF16),
            jax.ShapeDtypeStruct(wg.shape, BF16),
            jax.ShapeDtypeStruct(wu.shape, BF16),
            jax.ShapeDtypeStruct(wd.shape, BF16),
        ),
        in_specs=[src] * 8,
        out_specs=[vmem] * 2 + [hbm] * 3,
        scratch_shapes=[
            pltpu.VMEM((NZ, tok_rows, 2 * width), BF16),
            pltpu.VMEM((NZ, 16, tok_rows), F32),
            pltpu.VMEM((NZ, CH, 2 * width), BF16),
            pltpu.VMEM((NF, NZ * CH, 2 * width), BF16),
            pltpu.VMEM((NF, NZ * CH, 3 * hid), BF16),
            pltpu.VMEM((model, 2 * hid), BF16),
            pltpu.VMEM((NF, width, 2 * hid), BF16),
            pltpu.VMEM((NF, hid, width), BF16),
            pltpu.VMEM((NZ, CH, 2 * width), BF16),
            pltpu.VMEM((NZ, CH, 2 * width), BF16),
            pltpu.VMEM((2, NZ // 2, 2, tok_rows, width), BF16),
            pltpu.VMEM((2, NZ // 2, 2, tok_rows, width), BF16),
            pltpu.VMEM((CH, tok_rows), F32),
            pltpu.VMEM((NX, 16, tok_rows), F32),
            pltpu.VMEM((hid, model), BF16),
            pltpu.VMEM((model, 2 * hid), BF16),
            pltpu.VMEM((hid, model), BF16),
            pltpu.VMEM((8, 128), F32),
            pltpu.VMEM((NZ, tok_rows, 2 * CH), BF16),
            pltpu.VMEM((NZ, tok_rows, CH), BF16),
            pltpu.VMEM((model, hid), BF16),
            pltpu.VMEM((NF, 2 * hid, width), BF16),
            pltpu.VMEM((8, tok_rows), jnp.int32),
            pltpu.VMEM((8, tok_rows), jnp.int32),
            pltpu.VMEM((8, tok_rows), F32),
            dma((8,)),
            dma((3,)),
            dma((3,)),
            dma((3, NF)),
            dma((2, 2)),
            dma((2, 3, NZ // 2)),
            dma(()),
            dma((NZ, NX)),
            dma(()),
            dma((1, NX)),
            *gather_sems,
            *gather_sems,
            dma(()),
            dma((NZ, NX)),
            dma((2,)),
            dma((2, NZ // 2, 4)),
        ],
        compiler_params=pltpu.CompilerParams(
            collective_id=0, has_side_effects=True, vmem_limit_bytes=58 * 1024 * 1024
        ),
    )(tokens, output_grad, routes.T, kept_mask.T, gate_probs.T, wg, wu, wd)
    output, input_grad, g_gate, g_up, g_down = pl.pallas_call(
        functools.partial(put_out, len(outs)),
        out_shape=tuple(jax.ShapeDtypeStruct(o.shape, o.dtype) for o in outs),
        in_specs=[hbm] * 5,
        out_specs=[hbm] * 5,
        scratch_shapes=[pltpu.VMEM(o.shape, o.dtype) for o in outs] + [dma((2, 5))],
        compiler_params=pltpu.CompilerParams(vmem_limit_bytes=58 * 1024 * 1024),
    )(*outs)
    return output, input_grad, g_gate[None], g_up[None], g_down[None]


def solution(mesh):
    torus = Mesh(mesh.devices.reshape(NX, NZ, NY, NC), ("x", "z", "y", "c"))
    dp, expert = ("x", "z"), ("y", "c")
    return jax.shard_map(
        per_device,
        mesh=torus,
        in_specs=(
            P(dp, None),
            P(dp, None),
            P(dp, None),
            P(dp, None),
            P(dp, None),
            P(dp, None, expert),
            P(dp, None, expert),
            P(dp, expert, None),
        ),
        out_specs=(
            P(dp, expert),
            P(dp, expert),
            P(dp, None, expert),
            P(dp, None, expert),
            P(dp, expert, None),
        ),
        check_vma=False,
    )
```
